32 devices in a mesh: layer: 4 (over y, x), dp: 8 (over z, core).
Axes of the slice: x: 2, y: 2, z: 4, core: 2. Of those that a mesh axis runs over, the one named last changes fastest.
Arguments:
- x_in: bfloat16 [4, 320, 4096], P('layer', None, 'dp'), may hold values from -6 to 6
- enc_weight: bfloat16 [4, 4096, 256], P('layer', 'dp'), may hold values from -0.09375 to 0.09375
- active: int32 [4, 320, 256], P('layer'), may hold values 0 or 1
- dec_weight: bfloat16 [4, 4, 256, 4096], P('layer', None, None, 'dp'), may hold values from -0.1875 to 0.1875
- target: bfloat16 [4, 320, 4096], P('layer', None, 'dp'), may hold values from -6 to 6
- other_sum: bfloat16 [4, 320, 4096], P('layer', None, 'dp'), may hold values from -4 to 4
Outputs:
- dec_grad: float32 [4, 4, 256, 4096], P('layer', None, None, 'dp')
- enc_grad: float32 [4, 4096, 256], P('layer', 'dp')
The draws below stay inside these ranges and needn't reach their ends.
All inputs are finite; a program needn't handle non-finite values. No bound on the sum of `active` on one device may be relied on, other than what follows from the above.
Results may differ from the reference program's by a relative error of at most 0.018.
Values may be sent and summed in bfloat16 or wider, within the bound.
A program may use at most 64 MiB of HBM per device.

```python
import jax
import jax.numpy as jnp
from jax import lax

D = 4096
F = 256
TOKENS = 320
LAYERS = 4
N_DP = 8


def with_ends(result, key, low, largest):
    dims = result.shape
    place = [jax.random.randint(jax.random.fold_in(key, axis), (), 0, dims[axis]) for axis in range(len(dims))]
    result = result.at[tuple(place)].set(low)
    longest = dims.index(max(dims))
    place[longest] = (place[longest] + 1) % dims[longest]
    return result.at[tuple(place)].set(largest)


def block_scale(key, extent, split, least, largest):
    def one(dim, parts):
        heights = jax.random.uniform(jax.random.fold_in(jax.random.fold_in(key, 6), dim), (parts,), jnp.float32, least / len(split), largest / len(split))
        return jnp.repeat(jnp.exp(heights), extent[dim] // parts).reshape((-1,) + (1,) * (len(extent) - dim - 1))

    gain = one(*split[0])
    for cut in split[1:]:
        gain = gain * one(*cut)
    return gain


def gaussian(stream_key, dims, spread, most, split=(), kind=jnp.bfloat16):
    loudness = block_scale(stream_key, dims, split, -0.22, 0.18) if split else 1.0
    entries = jax.random.normal(stream_key, dims, jnp.float32) * spread * loudness
    return jnp.minimum(jnp.maximum(entries, -most), most).astype(kind)


def setup_inputs(seed: int = 0) -> dict:
    streams_of = jax.random.split(jax.random.key(seed), 7)
    return {
        "x_in": gaussian(streams_of[0], (LAYERS, TOKENS, D), 1.0, 6.0, ((0, 4), (2, 8))),
        "enc_weight": gaussian(streams_of[1], (LAYERS, D, F), D ** -0.5, 0.09375, ((0, 4), (1, 8))),
        "active": with_ends((jax.random.randint(streams_of[2], (LAYERS, TOKENS, F), 0, 8) < 3).astype(jnp.int32), jax.random.fold_in(streams_of[2], 1), 0, 1),
        "dec_weight": gaussian(streams_of[3], (LAYERS, LAYERS, F, D), (F * LAYERS) ** -0.5, 0.1875, ((0, 4), (3, 8))),
        "target": gaussian(streams_of[4], (LAYERS, TOKENS, D), 1.0, 6.0, ((0, 4), (2, 8))),
        "other_sum": gaussian(streams_of[5], (LAYERS, TOKENS, D), 0.5, 4.0, ((0, 4), (2, 8))),
    }


def rounded(value):
    return lax.optimization_barrier(value.astype(jnp.bfloat16)).astype(jnp.float32)


def reference(x_in, enc_weight, active, dec_weight, target, other_sum):
    inputs = x_in.astype(jnp.float32)
    pre = jnp.einsum("ltd,ldf->ltf", inputs, enc_weight.astype(jnp.float32))
    mask = active.astype(jnp.float32)
    latents = rounded(mask * pre)
    width = D // N_DP
    latent_grad = jnp.zeros((LAYERS, TOKENS, F), jnp.float32)
    dec_list = []
    for layer in range(LAYERS):
        used = latents[: layer + 1]
        decoder = dec_weight[layer, : layer + 1].astype(jnp.float32)
        recon = other_sum[layer].astype(jnp.float32) + jnp.einsum("stf,sfd->td", used, decoder)
        error = rounded(recon - target[layer].astype(jnp.float32))
        grads = jnp.einsum("stf,td->sfd", used, error)
        padding = jnp.zeros((LAYERS - layer - 1, F, D), jnp.float32)
        dec_list.append(jnp.concatenate([grads, padding], axis=0))

        def add_block(total, index):
            start = (index * width).astype(jnp.int32)
            err_block = lax.dynamic_slice_in_dim(error, start, width, 1)
            dec_block = lax.dynamic_slice_in_dim(decoder, start, width, 2)
            term = rounded(jnp.einsum("td,sfd->stf", err_block, dec_block))
            return total + term, None

        start_total = jnp.zeros((layer + 1, TOKENS, F), jnp.float32)
        summed, _ = lax.scan(add_block, start_total, jnp.arange(N_DP, dtype=jnp.int32))
        latent_grad = latent_grad.at[: layer + 1].add(summed)
    grad_pre = rounded(mask * latent_grad)
    enc_grad = jnp.einsum("ltd,ltf->ldf", inputs, grad_pre)
    return jnp.stack(dec_list), enc_grad
```

```python
import functools

import jax
import jax.numpy as jnp
from jax import lax
from jax.experimental import pallas as pl
from jax.experimental.pallas import tpu as pltpu
from jax.sharding import PartitionSpec as P

BF16 = jnp.bfloat16
F32 = jnp.float32


def loop(low, high, step):
    def one(index, carry):
        step(index)
        return carry

    lax.fori_loop(low, high, one, 0)


def kernel(
    dims, x_hbm, enc_hbm, act_hbm, dec_hbm, tgt_hbm, oth_hbm, dg_hbm, eg_hbm,
    x, enc, act, dec, tgt, oth, in_sem,
    pf, pb, pin, p_s, p_r,
    qs, qin, q_s, q_r,
    lat, zg_s, lf_s, lat_r, co_s, co_r,
    recon, err,
    tb, tp, tp_s, tp_r,
    cs, tr, tr_s, tr_r, lsf,
    ls, zr, z_s, z_r,
    g, g_s, g_r, gf_s, gf_r,
    dgv, egv, dg_sem, eg_sem,
):
    layers, chips, owners, rows, tokens, half = dims
    l = lax.axis_index("layer")
    d = lax.axis_index("dp")
    z = lax.div(d, 2)
    c = lax.rem(d, 2)
    other = 1 - c

    def owned(index, step):
        if owners == chips:
            step()
        else:
            pl.when(index < owners)(step)

    def span(k):
        return pl.ds(pl.multiple_of(k * rows, 16), rows)

    def peer(i):
        return lax.rem(z + i, chips)

    def remote(src, dst, send, recv, layer, part):
        return pltpu.make_async_remote_copy(
            src_ref=src, dst_ref=dst, send_sem=send, recv_sem=recv,
            device_id=(layer, part), device_id_type=pl.DeviceIdType.MESH,
        )

    def to_core(src, dst, send, recv):
        return remote(src, dst, send, recv, l, z * 2 + other)

    def to_chip(k, src, dst, send, recv):
        return remote(src, dst, send, recv, l, k * 2 + c)

    def to_layer(t, src, dst, send, recv):
        return remote(src, dst, send, recv, t, d)

    in_x = pltpu.make_async_copy(x_hbm.at[0], x, in_sem.at[0])
    in_enc = pltpu.make_async_copy(enc_hbm.at[0], enc, in_sem.at[1])
    in_dec = pltpu.make_async_copy(dec_hbm.at[0], dec, in_sem.at[2])
    in_tgt = pltpu.make_async_copy(tgt_hbm.at[0], tgt, in_sem.at[3])
    in_oth = pltpu.make_async_copy(oth_hbm.at[0], oth, in_sem.at[4])
    in_act = pltpu.make_async_copy(
        act_hbm.at[0, span(z), pl.ds(pl.multiple_of(c * half, 128), half)], act, in_sem.at[5]
    )
    in_x.start()
    in_enc.start()
    owned(z, in_act.start)
    in_oth.start()
    in_tgt.start()
    in_dec.start()

    barrier = pltpu.get_barrier_semaphore()

    def greet(layer, part):
        pl.semaphore_signal(
            barrier, inc=1, device_id=(layer, part), device_id_type=pl.DeviceIdType.MESH
        )

    greet(l, z * 2 + other)
    loop(1, chips, lambda i: greet(l, peer(i) * 2 + c))
    loop(1, layers, lambda i: greet(lax.rem(l + i, layers), d))

    in_x.wait()
    in_enc.wait()
    part = jnp.dot(x[...], enc[...], preferred_element_type=F32)
    pf[0] = part[:, :half]
    pf[1] = part[:, half:]
    pb[...] = pf[other].astype(BF16)
    pl.semaphore_wait(barrier, chips + layers - 1)

    pre_core = to_core(pb, pin, p_s, p_r)
    pre_core.start()

    def clear(s):
        dgv[s] = jnp.zeros_like(dgv[s])
        pltpu.make_async_copy(dgv.at[s], dg_hbm.at[0, s], dg_sem.at[s]).start()

    loop(l + 1, layers, clear)
    owned(z, in_act.wait)
    in_oth.wait()
    in_tgt.wait()
    recon[...] = oth[...].astype(F32) - tgt[...].astype(F32)
    pre_core.wait_recv()
    pf[c] = pf[c] + pin[...].astype(F32)
    qs[...] = pf[c].astype(BF16)

    def pre_copy(k, slot):
        return to_chip(k, qs.at[span(k)], qin.at[slot], q_s.at[k], q_r.at[slot])

    loop(1, chips, lambda i: owned(peer(i), pre_copy(peer(i), z).start))

    def lat_shard(s, k):
        return lat.at[s, c, span(k)]

    def lat_chip(k, slot):
        return to_chip(k, lat_shard(l, slot), lat_shard(l, slot), zg_s.at[k], lat_r.at[l, slot])

    def lat_layer(t, k):
        return to_layer(t, lat_shard(l, k), lat_shard(l, k), lf_s.at[t, k], lat_r.at[l, k])

    def lat_core(s):
        return to_core(lat.at[s, c], lat.at[s, c], co_s.at[s], co_r.at[s])

    def lat_wait(s, k):
        to_chip(z, lat_shard(s, k), lat_shard(s, k), zg_s.at[k], lat_r.at[s, k]).wait_recv()

    def own_latents():
        def add(i, total):
            k = peer(i)
            pre_copy(z, k).wait_recv()
            return total + qin[k].astype(F32)

        total = lax.fori_loop(1, chips, add, pf[c, span(z)])
        lat[l, c, span(z)] = (act[...].astype(F32) * total).astype(BF16)
        loop(1, chips, lambda i: lat_chip(peer(i), z).start())
        loop(l + 1, layers, lambda t: lat_layer(t, z).start())

    owned(z, own_latents)

    def pass_on(i):
        k = peer(i)

        def step():
            lat_wait(l, k)
            loop(l + 1, layers, lambda t: lat_layer(t, k).start())

        owned(k, step)

    loop(1, chips, pass_on)
    lat_core(l).start()
    in_dec.wait()

    def whole(ref):
        return jnp.concatenate([ref[0], ref[1]], axis=1)

    def add_source(s):
        to_core(lat.at[s, other], lat.at[s, other], co_s.at[s], co_r.at[s]).wait_recv()
        recon[...] += jnp.dot(whole(lat.at[s]), dec[s], preferred_element_type=F32)

    def take_source(i):
        s = l - 1 - i
        loop(0, owners, lambda k: lat_wait(s, k))
        lat_core(s).start()
        add_source(s + 1)

    loop(0, l, take_source)
    add_source(0)
    err[...] = recon[...].astype(BF16)

    def term_core(s, h):
        return to_core(tb.at[s, h], tp.at[s], tp_s.at[s], tp_r.at[s])

    def make_term(s):
        term = lax.dot_general(
            err[...], dec[s], (((1,), (1,)), ((), ())), preferred_element_type=F32
        ).astype(BF16)
        tb[s, 0] = term[:, :half]
        tb[s, 1] = term[:, half:]
        term_core(s, other).start()

    loop(0, l + 1, make_term)

    def term_layer(s, t, k):
        return to_layer(s, cs.at[s, span(k)], tr.at[t, span(k)], tr_s.at[s, k], tr_r.at[t, k])

    def join_term(s):
        term_core(s, c).wait_recv()
        cs[s] = (tb[s, c].astype(F32) + tp[s].astype(F32)).astype(BF16)
        loop(0, owners, lambda k: term_layer(s, l, k).start())

    loop(0, l, join_term)
    term_core(l, c).wait_recv()
    lsf[...] = tb[l, c].astype(F32) + tp[l].astype(F32)

    def make_grad(s):
        dgv[s] = lax.dot_general(
            whole(lat.at[s]), err[...], (((0,), (0,)), ((), ())), preferred_element_type=F32
        )
        pltpu.make_async_copy(dgv.at[s], dg_hbm.at[0, s], dg_sem.at[s]).start()

    loop(0, l + 1, make_grad)

    def sum_copy(k, slot):
        return to_chip(k, ls.at[span(k)], zr.at[slot], z_s.at[k], z_r.at[slot])

    def layer_sum(k):
        def add(t, total):
            term_layer(l, t, k).wait_recv()
            return total + tr[t, span(k)].astype(F32)

        return lax.fori_loop(l + 1, layers, add, lsf[span(k)])

    def reduce_chip(i):
        k = peer(i)

        def step():
            ls[span(k)] = layer_sum(k).astype(BF16)
            sum_copy(k, z).start()

        owned(k, step)

    loop(1, chips, reduce_chip)

    def g_chip(k, slot):
        return to_chip(k, g.at[c, span(slot)], g.at[c, span(slot)], g_s.at[k], g_r.at[slot])

    def g_core(k, h):
        return to_core(g.at[h, span(k)], g.at[h, span(k)], gf_s.at[k], gf_r.at[k])

    def own_grad():
        def add(i, total):
            k = peer(i)
            sum_copy(z, k).wait_recv()
            return total + zr[k].astype(F32)

        total = lax.fori_loop(1, chips, add, layer_sum(z))
        g[c, span(z)] = (act[...].astype(F32) * total).astype(BF16)
        loop(1, chips, lambda i: g_chip(peer(i), z).start())
        g_core(z, c).start()

    owned(z, own_grad)

    def g_pass(i):
        k = peer(i)

        def step():
            g_chip(z, k).wait_recv()
            g_core(k, c).start()

        owned(k, step)

    loop(1, chips, g_pass)
    loop(0, owners, lambda k: g_core(k, other).wait_recv())
    egv[...] = lax.dot_general(
        x[...], whole(g), (((0,), (0,)), ((), ())), preferred_element_type=F32
    )
    out = pltpu.make_async_copy(egv, eg_hbm.at[0], eg_sem)
    out.start()

    pre_core.wait_send()
    loop(1, chips, lambda i: owned(peer(i), pre_copy(peer(i), z).wait_send))

    def own_sends():
        loop(1, chips, lambda i: lat_chip(peer(i), z).wait_send())
        loop(1, chips, lambda i: g_chip(peer(i), z).wait_send())

    owned(z, own_sends)
    loop(l + 1, layers, lambda t: loop(0, owners, lambda k: lat_layer(t, k).wait_send()))
    loop(0, l + 1, lambda s: lat_core(s).wait_send())
    loop(0, l + 1, lambda s: term_core(s, other).wait_send())
    loop(0, l, lambda s: loop(0, owners, lambda k: term_layer(s, l, k).wait_send()))
    loop(1, chips, lambda i: owned(peer(i), sum_copy(peer(i), z).wait_send))
    loop(0, owners, lambda k: g_core(k, c).wait_send())
    loop(0, layers, lambda s: pltpu.make_async_copy(dgv.at[s], dg_hbm.at[0, s], dg_sem.at[s]).wait())
    out.wait()


def body(x_in, enc_weight, active, dec_weight, target, other_sum):
    layers = lax.axis_size("layer")
    chips = lax.axis_size("dp") // 2
    _, tokens, width = x_in.shape
    features = enc_weight.shape[2]
    half = features // 2
    rows = 16 * pl.cdiv(tokens, 16 * chips)
    owners = tokens // rows
    assert owners * rows == tokens and owners <= chips
    dims = (layers, chips, owners, rows, tokens, half)

    def sems(*shape):
        return pltpu.SemaphoreType.DMA(shape) if shape else pltpu.SemaphoreType.DMA

    V = pltpu.VMEM
    scratch = [
        V((tokens, width), BF16), V((width, features), BF16), V((rows, half), jnp.int32),
        V((layers, features, width), BF16), V((tokens, width), BF16), V((tokens, width), BF16), sems(6),
        V((2, tokens, half), F32), V((tokens, half), BF16), V((tokens, half), BF16), sems(), sems(),
        V((tokens, half), BF16), V((chips, rows, half), BF16), sems(chips), sems(chips),
        V((layers, 2, tokens, half), BF16), sems(chips), sems(layers, chips), sems(layers, chips),
        sems(layers), sems(layers),
        V((tokens, width), F32), V((tokens, width), BF16),
        V((layers, 2, tokens, half), BF16), V((layers, tokens, half), BF16), sems(layers), sems(layers),
        V((layers, tokens, half), BF16), V((layers, tokens, half), BF16), sems(layers, chips),
        sems(layers, chips), V((tokens, half), F32),
        V((tokens, half), BF16), V((chips, rows, half), BF16), sems(chips), sems(chips),
        V((2, tokens, half), BF16), sems(chips), sems(chips), sems(chips), sems(chips),
        V((layers, features, width), F32), V((width, features), F32), sems(layers), sems(),
    ]
    return pl.pallas_call(
        functools.partial(kernel, dims),
        out_shape=(
            jax.ShapeDtypeStruct((1, layers, features, width), F32),
            jax.ShapeDtypeStruct((1, width, features), F32),
        ),
        in_specs=[pl.BlockSpec(memory_space=pl.ANY)] * 6,
        out_specs=[pl.BlockSpec(memory_space=pl.ANY)] * 2,
        scratch_shapes=scratch,
        compiler_params=pltpu.CompilerParams(
            collective_id=0, has_side_effects=True, vmem_limit_bytes=48 * 1024 * 1024
        ),
    )(x_in, enc_weight, active, dec_weight, target, other_sum)


def solution(mesh):
    return jax.shard_map(
        body,
        mesh=mesh,
        in_specs=(
            P("layer", None, "dp"),
            P("layer", "dp", None),
            P("layer", None, None),
            P("layer", None, None, "dp"),
            P("layer", None, "dp"),
            P("layer", None, "dp"),
        ),
        out_specs=(P("layer", None, None, "dp"), P("layer", "dp", None)),
        check_vma=False,
    )
```

```python
import functools

import jax
import jax.numpy as jnp
from jax import lax
from jax.experimental import pallas as pl
from jax.experimental.pallas import tpu as pltpu
from jax.sharding import PartitionSpec as P

BF16 = jnp.bfloat16
F32 = jnp.float32


def loop(low, high, step):
    def one(index, carry):
        step(index)
        return carry

    lax.fori_loop(low, high, one, 0)


def kernel(
    dims, x_hbm, enc_hbm, act_hbm, dec_hbm, tgt_hbm, oth_hbm, dg_hbm, g_out,
    x, enc, act, dec, tgt, oth, in_sem,
    pf, pb, pin, p_s, p_r,
    qs, qin, q_s, q_r,
    lat, zg_s, lf_s, lat_r, co_s, co_r,
    recon, err,
    tb, tp, tp_s, tp_r,
    cs, tr, tr_s, tr_r, lsf,
    ls, zr, z_s, z_r,
    g, g_s, g_r, gf_s, gf_r,
    dgv, dg_sem, g_sem,
):
    layers, chips, owners, rows, tokens, half = dims
    l = lax.axis_index("layer")
    d = lax.axis_index("dp")
    z = lax.div(d, 2)
    c = lax.rem(d, 2)
    other = 1 - c

    def owned(index, step):
        if owners == chips:
            step()
        else:
            pl.when(index < owners)(step)

    def span(k):
        return pl.ds(pl.multiple_of(k * rows, 16), rows)

    def peer(i):
        return lax.rem(z + i, chips)

    def remote(src, dst, send, recv, layer, part):
        return pltpu.make_async_remote_copy(
            src_ref=src, dst_ref=dst, send_sem=send, recv_sem=recv,
            device_id=(layer, part), device_id_type=pl.DeviceIdType.MESH,
        )

    def to_core(src, dst, send, recv):
        return remote(src, dst, send, recv, l, z * 2 + other)

    def to_chip(k, src, dst, send, recv):
        return remote(src, dst, send, recv, l, k * 2 + c)

    def to_layer(t, src, dst, send, recv):
        return remote(src, dst, send, recv, t, d)

    in_x = pltpu.make_async_copy(x_hbm.at[0], x, in_sem.at[0])
    in_enc = pltpu.make_async_copy(enc_hbm.at[0], enc, in_sem.at[1])
    in_dec = pltpu.make_async_copy(dec_hbm.at[0], dec, in_sem.at[2])
    in_tgt = pltpu.make_async_copy(tgt_hbm.at[0], tgt, in_sem.at[3])
    in_oth = pltpu.make_async_copy(oth_hbm.at[0], oth, in_sem.at[4])
    in_act = pltpu.make_async_copy(
        act_hbm.at[0, span(z), pl.ds(pl.multiple_of(c * half, 128), half)], act, in_sem.at[5]
    )
    in_x.start()
    in_enc.start()
    owned(z, in_act.start)
    in_oth.start()
    in_tgt.start()
    in_dec.start()

    barrier = pltpu.get_barrier_semaphore()

    def greet(layer, part):
        pl.semaphore_signal(
            barrier, inc=1, device_id=(layer, part), device_id_type=pl.DeviceIdType.MESH
        )

    greet(l, z * 2 + other)
    loop(1, chips, lambda i: greet(l, peer(i) * 2 + c))
    loop(1, layers, lambda i: greet(lax.rem(l + i, layers), d))

    in_x.wait()
    in_enc.wait()
    part = jnp.dot(x[...], enc[...], preferred_element_type=F32)
    pf[0] = part[:, :half]
    pf[1] = part[:, half:]
    pb[...] = pf[other].astype(BF16)
    pl.semaphore_wait(barrier, chips + layers - 1)

    pre_core = to_core(pb, pin, p_s, p_r)
    pre_core.start()

    def clear(s):
        dgv[s] = jnp.zeros_like(dgv[s])
        pltpu.make_async_copy(dgv.at[s], dg_hbm.at[0, s], dg_sem.at[s]).start()

    loop(l + 1, layers, clear)
    owned(z, in_act.wait)
    in_oth.wait()
    in_tgt.wait()
    recon[...] = oth[...].astype(F32) - tgt[...].astype(F32)
    pre_core.wait_recv()
    pf[c] = pf[c] + pin[...].astype(F32)
    qs[...] = pf[c].astype(BF16)

    def pre_copy(k, slot):
        return to_chip(k, qs.at[span(k)], qin.at[slot], q_s.at[k], q_r.at[slot])

    loop(1, chips, lambda i: owned(peer(i), pre_copy(peer(i), z).start))

    def lat_shard(s, k):
        return lat.at[s, c, span(k)]

    def lat_chip(k, slot):
        return to_chip(k, lat_shard(l, slot), lat_shard(l, slot), zg_s.at[k], lat_r.at[l, slot])

    def lat_layer(t, k):
        return to_layer(t, lat_shard(l, k), lat_shard(l, k), lf_s.at[t, k], lat_r.at[l, k])

    def lat_core(s):
        return to_core(lat.at[s, c], lat.at[s, c], co_s.at[s], co_r.at[s])

    def lat_wait(s, k):
        to_chip(z, lat_shard(s, k), lat_shard(s, k), zg_s.at[k], lat_r.at[s, k]).wait_recv()

    def own_latents():
        def add(i, total):
            k = peer(i)
            pre_copy(z, k).wait_recv()
            return total + qin[k].astype(F32)

        total = lax.fori_loop(1, chips, add, pf[c, span(z)])
        lat[l, c, span(z)] = (act[...].astype(F32) * total).astype(BF16)
        loop(1, chips, lambda i: lat_chip(peer(i), z).start())
        loop(l + 1, layers, lambda t: lat_layer(t, z).start())

    owned(z, own_latents)

    def pass_on(i):
        k = peer(i)

        def step():
            lat_wait(l, k)
            loop(l + 1, layers, lambda t: lat_layer(t, k).start())

        owned(k, step)

    loop(1, chips, pass_on)
    lat_core(l).start()
    in_dec.wait()

    def whole(ref):
        return jnp.concatenate([ref[0], ref[1]], axis=1)

    def add_source(s):
        to_core(lat.at[s, other], lat.at[s, other], co_s.at[s], co_r.at[s]).wait_recv()
        recon[...] += jnp.dot(whole(lat.at[s]), dec[s], preferred_element_type=F32)

    def take_source(i):
        s = l - 1 - i
        loop(0, owners, lambda k: lat_wait(s, k))
        lat_core(s).start()
        add_source(s + 1)

    loop(0, l, take_source)
    add_source(0)
    err[...] = recon[...].astype(BF16)

    def term_core(s, h):
        return to_core(tb.at[s, h], tp.at[s], tp_s.at[s], tp_r.at[s])

    def make_term(s):
        term = lax.dot_general(
            err[...], dec[s], (((1,), (1,)), ((), ())), preferred_element_type=F32
        ).astype(BF16)
        tb[s, 0] = term[:, :half]
        tb[s, 1] = term[:, half:]
        term_core(s, other).start()

    loop(0, l + 1, make_term)

    def term_layer(s, t, k):
        return to_layer(s, cs.at[s, span(k)], tr.at[t, span(k)], tr_s.at[s, k], tr_r.at[t, k])

    def join_term(s):
        term_core(s, c).wait_recv()
        cs[s] = (tb[s, c].astype(F32) + tp[s].astype(F32)).astype(BF16)
        loop(0, owners, lambda k: term_layer(s, l, k).start())

    loop(0, l, join_term)
    term_core(l, c).wait_recv()
    lsf[...] = tb[l, c].astype(F32) + tp[l].astype(F32)

    def make_grad(s):
        dgv[s] = lax.dot_general(
            whole(lat.at[s]), err[...], (((0,), (0,)), ((), ())), preferred_element_type=F32
        )
        pltpu.make_async_copy(dgv.at[s], dg_hbm.at[0, s], dg_sem.at[s]).start()

    loop(0, l + 1, make_grad)

    def sum_copy(k, slot):
        return to_chip(k, ls.at[span(k)], zr.at[slot], z_s.at[k], z_r.at[slot])

    def layer_sum(k):
        def add(t, total):
            term_layer(l, t, k).wait_recv()
            return total + tr[t, span(k)].astype(F32)

        return lax.fori_loop(l + 1, layers, add, lsf[span(k)])

    def reduce_chip(i):
        k = peer(i)

        def step():
            ls[span(k)] = layer_sum(k).astype(BF16)
            sum_copy(k, z).start()

        owned(k, step)

    loop(1, chips, reduce_chip)

    def g_chip(k, slot):
        return to_chip(k, g.at[c, span(slot)], g.at[c, span(slot)], g_s.at[k], g_r.at[slot])

    def g_core(k, h):
        return to_core(g.at[h, span(k)], g.at[h, span(k)], gf_s.at[k], gf_r.at[k])

    def own_grad():
        def add(i, total):
            k = peer(i)
            sum_copy(z, k).wait_recv()
            return total + zr[k].astype(F32)

        total = lax.fori_loop(1, chips, add, layer_sum(z))
        g[c, span(z)] = (act[...].astype(F32) * total).astype(BF16)
        loop(1, chips, lambda i: g_chip(peer(i), z).start())
        g_core(z, c).start()

    owned(z, own_grad)

    def g_pass(i):
        k = peer(i)

        def step():
            g_chip(z, k).wait_recv()
            g_core(k, c).start()

        owned(k, step)

    loop(1, chips, g_pass)
    loop(0, owners, lambda k: g_core(k, other).wait_recv())
    out = pltpu.make_async_copy(g, g_out, g_sem)
    out.start()

    pre_core.wait_send()
    loop(1, chips, lambda i: owned(peer(i), pre_copy(peer(i), z).wait_send))

    def own_sends():
        loop(1, chips, lambda i: lat_chip(peer(i), z).wait_send())
        loop(1, chips, lambda i: g_chip(peer(i), z).wait_send())

    owned(z, own_sends)
    loop(l + 1, layers, lambda t: loop(0, owners, lambda k: lat_layer(t, k).wait_send()))
    loop(0, l + 1, lambda s: lat_core(s).wait_send())
    loop(0, l + 1, lambda s: term_core(s, other).wait_send())
    loop(0, l, lambda s: loop(0, owners, lambda k: term_layer(s, l, k).wait_send()))
    loop(1, chips, lambda i: owned(peer(i), sum_copy(peer(i), z).wait_send))
    loop(0, owners, lambda k: g_core(k, c).wait_send())
    loop(0, layers, lambda s: pltpu.make_async_copy(dgv.at[s], dg_hbm.at[0, s], dg_sem.at[s]).wait())
    out.wait()


def body(x_in, enc_weight, active, dec_weight, target, other_sum):
    layers = lax.axis_size("layer")
    chips = lax.axis_size("dp") // 2
    _, tokens, width = x_in.shape
    features = enc_weight.shape[2]
    half = features // 2
    rows = 16 * pl.cdiv(tokens, 16 * chips)
    owners = tokens // rows
    assert owners * rows == tokens and owners <= chips
    dims = (layers, chips, owners, rows, tokens, half)

    def sems(*shape):
        return pltpu.SemaphoreType.DMA(shape) if shape else pltpu.SemaphoreType.DMA

    V = pltpu.VMEM
    scratch = [
        V((tokens, width), BF16), V((width, features), BF16), V((rows, half), jnp.int32),
        V((layers, features, width), BF16), V((tokens, width), BF16), V((tokens, width), BF16), sems(6),
        V((2, tokens, half), F32), V((tokens, half), BF16), V((tokens, half), BF16), sems(), sems(),
        V((tokens, half), BF16), V((chips, rows, half), BF16), sems(chips), sems(chips),
        V((layers, 2, tokens, half), BF16), sems(chips), sems(layers, chips), sems(layers, chips),
        sems(layers), sems(layers),
        V((tokens, width), F32), V((tokens, width), BF16),
        V((layers, 2, tokens, half), BF16), V((layers, tokens, half), BF16), sems(layers), sems(layers),
        V((layers, tokens, half), BF16), V((layers, tokens, half), BF16), sems(layers, chips),
        sems(layers, chips), V((tokens, half), F32),
        V((tokens, half), BF16), V((chips, rows, half), BF16), sems(chips), sems(chips),
        V((2, tokens, half), BF16), sems(chips), sems(chips), sems(chips), sems(chips),
        V((layers, features, width), F32), sems(layers), sems(),
    ]
    dec_grad, grad_pre = pl.pallas_call(
        functools.partial(kernel, dims),
        out_shape=(
            jax.ShapeDtypeStruct((1, layers, features, width), F32),
            jax.ShapeDtypeStruct((2, tokens, half), BF16),
        ),
        in_specs=[pl.BlockSpec(memory_space=pltpu.HBM)] * 6,
        out_specs=[pl.BlockSpec(memory_space=pl.ANY)] * 2,
        scratch_shapes=scratch,
        compiler_params=pltpu.CompilerParams(
            collective_id=0, has_side_effects=True, vmem_limit_bytes=48 * 1024 * 1024
        ),
    )(x_in, enc_weight, active, dec_weight, target, other_sum)
    grad_pre = jnp.concatenate([grad_pre[0], grad_pre[1]], axis=1)
    enc_grad = jnp.einsum("td,tf->df", x_in[0], grad_pre, preferred_element_type=F32)
    return dec_grad, enc_grad[None]


def solution(mesh):
    return jax.shard_map(
        body,
        mesh=mesh,
        in_specs=(
            P("layer", None, "dp"),
            P("layer", "dp", None),
            P("layer", None, None),
            P("layer", None, None, "dp"),
            P("layer", None, "dp"),
            P("layer", None, "dp"),
        ),
        out_specs=(P("layer", None, None, "dp"), P("layer", "dp", None)),
        check_vma=False,
    )
```

```python
import functools

import jax
import jax.numpy as jnp
from jax import lax
from jax.experimental import pallas as pl
from jax.experimental.pallas import tpu as pltpu
from jax.sharding import PartitionSpec as P

BF16 = jnp.bfloat16
F32 = jnp.float32


def loop(low, high, step):
    def one(index, carry):
        step(index)
        return carry

    lax.fori_loop(low, high, one, 0)


def kernel(
    dims, x_hbm, enc_hbm, act_hbm, dec_hbm, tgt_hbm, oth_hbm, dg_hbm, eg_hbm,
    x, enc, act, dec, tgt, oth, in_sem,
    pf, pb, pin, p_s, p_r,
    qs, qin, q_s, q_r,
    lat, zg_s, lf_s, lat_r, co_s, co_r,
    recon, err,
    tb, tp, tp_s, tp_r,
    cs, tr, tr_s, tr_r, lsf,
    ls, zr, z_s, z_r,
    g, g_s, g_r, gf_s, gf_r,
    dgv, egv, dg_sem, eg_sem,
):
    layers, chips, owners, rows, tokens, half = dims
    l = lax.axis_index("layer")
    d = lax.axis_index("dp")
    z = lax.div(d, 2)
    c = lax.rem(d, 2)
    other = 1 - c

    def owned(index, step):
        if owners == chips:
            step()
        else:
            pl.when(index < owners)(step)

    def span(k):
        return pl.ds(pl.multiple_of(k * rows, 16), rows)

    def peer(i):
        return lax.rem(z + i, chips)

    def remote(src, dst, send, recv, layer, part):
        return pltpu.make_async_remote_copy(
            src_ref=src, dst_ref=dst, send_sem=send, recv_sem=recv,
            device_id=(layer, part), device_id_type=pl.DeviceIdType.MESH,
        )

    def to_core(src, dst, send, recv):
        return remote(src, dst, send, recv, l, z * 2 + other)

    def to_chip(k, src, dst, send, recv):
        return remote(src, dst, send, recv, l, k * 2 + c)

    def to_layer(t, src, dst, send, recv):
        return remote(src, dst, send, recv, t, d)

    in_x = pltpu.make_async_copy(x_hbm.at[0], x, in_sem.at[0])
    in_enc = pltpu.make_async_copy(enc_hbm.at[0], enc, in_sem.at[1])
    in_dec = pltpu.make_async_copy(dec_hbm.at[0], dec, in_sem.at[2])
    in_tgt = pltpu.make_async_copy(tgt_hbm.at[0], tgt, in_sem.at[3])
    in_oth = pltpu.make_async_copy(oth_hbm.at[0], oth, in_sem.at[4])
    in_act = pltpu.make_async_copy(
        act_hbm.at[0, span(z), pl.ds(pl.multiple_of(c * half, 128), half)], act, in_sem.at[5]
    )
    in_x.start()
    in_enc.start()
    owned(z, in_act.start)
    in_oth.start()
    in_tgt.start()
    in_dec.start()

    barrier = pltpu.get_barrier_semaphore()

    def greet(layer, part):
        pl.semaphore_signal(
            barrier, inc=1, device_id=(layer, part), device_id_type=pl.DeviceIdType.MESH
        )

    greet(l, z * 2 + other)
    loop(1, chips, lambda i: greet(l, peer(i) * 2 + c))
    loop(1, layers, lambda i: greet(lax.rem(l + i, layers), d))

    in_x.wait()
    in_enc.wait()
    part = jnp.dot(x[...], enc[...], preferred_element_type=F32)
    pf[0] = part[:, :half]
    pf[1] = part[:, half:]
    pb[...] = pf[other].astype(BF16)
    pl.semaphore_wait(barrier, chips + layers - 1)

    pre_core = to_core(pb, pin, p_s, p_r)
    pre_core.start()

    def clear(s):
        dgv[s] = jnp.zeros_like(dgv[s])
        pltpu.make_async_copy(dgv.at[s], dg_hbm.at[0, s], dg_sem.at[s]).start()

    loop(l + 1, layers, clear)
    owned(z, in_act.wait)
    in_oth.wait()
    in_tgt.wait()
    recon[...] = oth[...].astype(F32) - tgt[...].astype(F32)
    pre_core.wait_recv()
    pf[c] = pf[c] + pin[...].astype(F32)
    qs[...] = pf[c].astype(BF16)

    def pre_copy(k, slot):
        return to_chip(k, qs.at[span(k)], qin.at[slot], q_s.at[k], q_r.at[slot])

    loop(1, chips, lambda i: owned(peer(i), pre_copy(peer(i), z).start))

    def lat_shard(s, k):
        return lat.at[s, c, span(k)]

    def lat_chip(k, slot):
        return to_chip(k, lat_shard(l, slot), lat_shard(l, slot), zg_s.at[k], lat_r.at[l, slot])

    def lat_layer(t, k):
        return to_layer(t, lat_shard(l, k), lat_shard(l, k), lf_s.at[t, k], lat_r.at[l, k])

    def lat_core(s):
        return to_core(lat.at[s, c], lat.at[s, c], co_s.at[s], co_r.at[s])

    def lat_wait(s, k):
        to_chip(z, lat_shard(s, k), lat_shard(s, k), zg_s.at[k], lat_r.at[s, k]).wait_recv()

    def own_latents():
        def add(i, total):
            k = peer(i)
            pre_copy(z, k).wait_recv()
            return total + qin[k].astype(F32)

        total = lax.fori_loop(1, chips, add, pf[c, span(z)])
        lat[l, c, span(z)] = (act[...].astype(F32) * total).astype(BF16)
        loop(1, chips, lambda i: lat_chip(peer(i), z).start())
        loop(l + 1, layers, lambda t: lat_layer(t, z).start())

    owned(z, own_latents)

    def pass_on(i):
        k = peer(i)

        def step():
            lat_wait(l, k)
            loop(l + 1, layers, lambda t: lat_layer(t, k).start())

        owned(k, step)

    loop(1, chips, pass_on)
    lat_core(l).start()
    in_dec.wait()

    def whole(ref):
        return jnp.concatenate([ref[0], ref[1]], axis=1)

    def add_source(s):
        to_core(lat.at[s, other], lat.at[s, other], co_s.at[s], co_r.at[s]).wait_recv()
        recon[...] += jnp.dot(whole(lat.at[s]), dec[s], preferred_element_type=F32)

    def take_source(i):
        s = l - 1 - i
        loop(0, owners, lambda k: lat_wait(s, k))
        lat_core(s).start()
        add_source(s + 1)

    loop(0, l, take_source)
    add_source(0)
    err[...] = recon[...].astype(BF16)

    def term_core(s, h):
        return to_core(tb.at[s, h], tp.at[s], tp_s.at[s], tp_r.at[s])

    def make_term(s):
        term = lax.dot_general(
            err[...], dec[s], (((1,), (1,)), ((), ())), preferred_element_type=F32
        ).astype(BF16)
        tb[s, 0] = term[:, :half]
        tb[s, 1] = term[:, half:]
        term_core(s, other).start()

    loop(0, l + 1, make_term)

    def term_layer(s, t, k):
        return to_layer(s, cs.at[s, span(k)], tr.at[t, span(k)], tr_s.at[s, k], tr_r.at[t, k])

    def join_term(s):
        term_core(s, c).wait_recv()
        cs[s] = (tb[s, c].astype(F32) + tp[s].astype(F32)).astype(BF16)
        loop(0, owners, lambda k: term_layer(s, l, k).start())

    loop(0, l, join_term)
    term_core(l, c).wait_recv()
    lsf[...] = tb[l, c].astype(F32) + tp[l].astype(F32)

    def make_grad(s):
        dgv[s] = lax.dot_general(
            whole(lat.at[s]), err[...], (((0,), (0,)), ((), ())), preferred_element_type=F32
        )
        pltpu.make_async_copy(dgv.at[s], dg_hbm.at[0, s], dg_sem.at[s]).start()

    loop(0, l + 1, make_grad)

    def sum_copy(k, slot):
        return to_chip(k, ls.at[span(k)], zr.at[slot], z_s.at[k], z_r.at[slot])

    def layer_sum(k):
        def add(t, total):
            term_layer(l, t, k).wait_recv()
            return total + tr[t, span(k)].astype(F32)

        return lax.fori_loop(l + 1, layers, add, lsf[span(k)])

    def reduce_chip(i):
        k = peer(i)

        def step():
            ls[span(k)] = layer_sum(k).astype(BF16)
            sum_copy(k, z).start()

        owned(k, step)

    loop(1, chips, reduce_chip)

    def g_chip(k, slot):
        return to_chip(k, g.at[c, span(slot)], g.at[c, span(slot)], g_s.at[k], g_r.at[slot])

    def g_core(k, h):
        return to_core(g.at[h, span(k)], g.at[h, span(k)], gf_s.at[k], gf_r.at[k])

    def own_grad():
        def add(i, total):
            k = peer(i)
            sum_copy(z, k).wait_recv()
            return total + zr[k].astype(F32)

        total = lax.fori_loop(1, chips, add, layer_sum(z))
        g[c, span(z)] = (act[...].astype(F32) * total).astype(BF16)
        loop(1, chips, lambda i: g_chip(peer(i), z).start())
        g_core(z, c).start()

    owned(z, own_grad)

    def g_pass(i):
        k = peer(i)

        def step():
            g_chip(z, k).wait_recv()
            g_core(k, c).start()

        owned(k, step)

    loop(1, chips, g_pass)
    loop(0, owners, lambda k: g_core(k, other).wait_recv())
    egv[...] = lax.dot_general(
        x[...], whole(g), (((0,), (0,)), ((), ())), preferred_element_type=F32
    )
    out = pltpu.make_async_copy(egv, eg_hbm.at[0], eg_sem)
    out.start()

    pre_core.wait_send()
    loop(1, chips, lambda i: owned(peer(i), pre_copy(peer(i), z).wait_send))

    def own_sends():
        loop(1, chips, lambda i: lat_chip(peer(i), z).wait_send())
        loop(1, chips, lambda i: g_chip(peer(i), z).wait_send())

    owned(z, own_sends)
    loop(l + 1, layers, lambda t: loop(0, owners, lambda k: lat_layer(t, k).wait_send()))
    loop(0, l + 1, lambda s: lat_core(s).wait_send())
    loop(0, l + 1, lambda s: term_core(s, other).wait_send())
    loop(0, l, lambda s: loop(0, owners, lambda k: term_layer(s, l, k).wait_send()))
    loop(1, chips, lambda i: owned(peer(i), sum_copy(peer(i), z).wait_send))
    loop(0, owners, lambda k: g_core(k, c).wait_send())
    loop(0, layers, lambda s: pltpu.make_async_copy(dgv.at[s], dg_hbm.at[0, s], dg_sem.at[s]).wait())
    out.wait()


def body(x_in, enc_weight, active, dec_weight, target, other_sum):
    layers = lax.axis_size("layer")
    chips = lax.axis_size("dp") // 2
    _, tokens, width = x_in.shape
    features = enc_weight.shape[2]
    half = features // 2
    rows = 16 * pl.cdiv(tokens, 16 * chips)
    owners = tokens // rows
    assert owners * rows == tokens and owners <= chips
    dims = (layers, chips, owners, rows, tokens, half)

    def sems(*shape):
        return pltpu.SemaphoreType.DMA(shape) if shape else pltpu.SemaphoreType.DMA

    V = pltpu.VMEM
    scratch = [
        V((tokens, width), BF16), V((width, features), BF16), V((rows, half), jnp.int32),
        V((layers, features, width), BF16), V((tokens, width), BF16), V((tokens, width), BF16), sems(6),
        V((2, tokens, half), F32), V((tokens, half), BF16), V((tokens, half), BF16), sems(), sems(),
        V((tokens, half), BF16), V((chips, rows, half), BF16), sems(chips), sems(chips),
        V((layers, 2, tokens, half), BF16), sems(chips), sems(layers, chips), sems(layers, chips),
        sems(layers), sems(layers),
        V((tokens, width), F32), V((tokens, width), BF16),
        V((layers, 2, tokens, half), BF16), V((layers, tokens, half), BF16), sems(layers), sems(layers),
        V((layers, tokens, half), BF16), V((layers, tokens, half), BF16), sems(layers, chips),
        sems(layers, chips), V((tokens, half), F32),
        V((tokens, half), BF16), V((chips, rows, half), BF16), sems(chips), sems(chips),
        V((2, tokens, half), BF16), sems(chips), sems(chips), sems(chips), sems(chips),
        V((layers, features, width), F32), V((width, features), F32), sems(layers), sems(),
    ]
    return pl.pallas_call(
        functools.partial(kernel, dims),
        out_shape=(
            jax.ShapeDtypeStruct((1, layers, features, width), F32),
            jax.ShapeDtypeStruct((1, width, features), F32),
        ),
        in_specs=[pl.BlockSpec(memory_space=pl.ANY)] * 6,
        out_specs=[pl.BlockSpec(memory_space=pl.ANY)] * 2,
        scratch_shapes=scratch,
        compiler_params=pltpu.CompilerParams(
            collective_id=0, has_side_effects=True, vmem_limit_bytes=63 * 1024 * 1024
        ),
    )(x_in, enc_weight, active, dec_weight, target, other_sum)


def solution(mesh):
    return jax.shard_map(
        body,
        mesh=mesh,
        in_specs=(
            P("layer", None, "dp"),
            P("layer", "dp", None),
            P("layer", None, None),
            P("layer", None, None, "dp"),
            P("layer", None, "dp"),
            P("layer", None, "dp"),
        ),
        out_specs=(P("layer", None, None, "dp"), P("layer", "dp", None)),
        check_vma=False,
    )
```

```python
import functools

import jax
import jax.numpy as jnp
from jax import lax
from jax.experimental import pallas as pl
from jax.experimental.pallas import tpu as pltpu
from jax.sharding import PartitionSpec as P

BF16 = jnp.bfloat16
F32 = jnp.float32
REACH = 3


def loop(low, high, step):
    def one(index, carry):
        step(index)
        return carry

    lax.fori_loop(low, high, one, 0)


def kernel(
    dims, x_hbm, enc_hbm, act_hbm, dec_hbm, tgt_hbm, oth_hbm, dg_hbm, eg_hbm,
    x, enc, act, dec, tgt, oth, in_sem,
    pf, pb, pin, p_s, p_r,
    qs, qin, q_s, q_r,
    lat, zg_s, lf_s, ld_s, lat_r, co_s, co_r,
    recon, err,
    tb, tp, tp_s, tp_r,
    cs, tr, tr_s, tr_r, td, td_r, lsf,
    ls, zr, z_s, z_r,
    g, g_s, g_r, gf_s, gf_r, gd_s,
    dgv, egv, dg_sem, eg_sem,
):
    layers, chips, owners, rows, tokens, half = dims
    l = lax.axis_index("layer")
    d = lax.axis_index("dp")
    z = lax.div(d, 2)
    c = lax.rem(d, 2)
    other = 1 - c

    def owned(index, step):
        if owners == chips:
            step()
        else:
            pl.when(index < owners)(step)

    def span(k):
        return pl.ds(pl.multiple_of(k * rows, 16), rows)

    lower = 2 * z < chips
    place = jnp.where(lower, chips - 1 - z, z)

    def far(j):
        j = j + jnp.where(j >= place, 1, 0)
        return jnp.where(lower, chips - 1 - j, j)

    def peers(step):
        loop(0, chips - 1, lambda j: step(far(j)))

    def peers_near_first(step):
        loop(0, chips - 1, lambda j: step(far(chips - 2 - j)))

    def distant(k):
        return jnp.abs(k - z) >= REACH

    def if_distant(k, step):
        if chips > REACH:
            pl.when(distant(k))(step)

    def if_close(k, step):
        if chips > REACH:
            pl.when(jnp.logical_not(distant(k)))(step)
        else:
            step()

    far_count = jnp.maximum(z - REACH + 1, 0) + jnp.maximum(chips - REACH - z, 0)

    def remote(src, dst, send, recv, layer, part):
        return pltpu.make_async_remote_copy(
            src_ref=src, dst_ref=dst, send_sem=send, recv_sem=recv,
            device_id=(layer, part), device_id_type=pl.DeviceIdType.MESH,
        )

    def to_core(src, dst, send, recv):
        return remote(src, dst, send, recv, l, z * 2 + other)

    def to_chip(k, src, dst, send, recv):
        return remote(src, dst, send, recv, l, k * 2 + c)

    def to_layer(t, src, dst, send, recv):
        return remote(src, dst, send, recv, t, d)

    in_x = pltpu.make_async_copy(x_hbm.at[0], x, in_sem.at[0])
    in_enc = pltpu.make_async_copy(enc_hbm.at[0], enc, in_sem.at[1])
    in_dec = pltpu.make_async_copy(dec_hbm.at[0], dec, in_sem.at[2])
    in_tgt = pltpu.make_async_copy(tgt_hbm.at[0], tgt, in_sem.at[3])
    in_oth = pltpu.make_async_copy(oth_hbm.at[0], oth, in_sem.at[4])
    in_act = pltpu.make_async_copy(
        act_hbm.at[0, span(z), pl.ds(pl.multiple_of(c * half, 128), half)], act, in_sem.at[5]
    )
    in_x.start()
    in_enc.start()
    owned(z, in_act.start)
    in_oth.start()
    in_tgt.start()
    in_dec.start()

    barrier = pltpu.get_barrier_semaphore()

    def greet(layer, part):
        pl.semaphore_signal(
            barrier, inc=1, device_id=(layer, part), device_id_type=pl.DeviceIdType.MESH
        )

    greet(l, z * 2 + other)
    peers(lambda k: greet(l, k * 2 + c))
    loop(1, layers, lambda i: greet(lax.rem(l + i, layers), d))

    def greet_distant(k):
        greet(l, k * 2 + other)
        loop(1, layers, lambda i: greet(lax.rem(l + i, layers), k * 2 + c))

    peers(lambda k: if_distant(k, lambda: greet_distant(k)))

    in_x.wait()
    in_enc.wait()
    part = jnp.dot(x[...], enc[...], preferred_element_type=F32)
    pf[0] = part[:, :half]
    pf[1] = part[:, half:]
    pb[...] = pf[other].astype(BF16)
    pl.semaphore_wait(barrier, chips + layers - 1 + far_count * layers)

    pre_core = to_core(pb, pin, p_s, p_r)
    pre_core.start()

    def clear(s):
        dgv[s] = jnp.zeros_like(dgv[s])
        pltpu.make_async_copy(dgv.at[s], dg_hbm.at[0, s], dg_sem.at[s]).start()

    loop(l + 1, layers, clear)
    owned(z, in_act.wait)
    in_oth.wait()
    in_tgt.wait()
    recon[...] = oth[...].astype(F32) - tgt[...].astype(F32)
    pre_core.wait_recv()
    pf[c] = pf[c] + pin[...].astype(F32)
    qs[...] = pf[c].astype(BF16)

    def pre_copy(k, slot):
        return to_chip(k, qs.at[span(k)], qin.at[slot], q_s.at[k], q_r.at[slot])

    peers(lambda k: owned(k, pre_copy(k, z).start))

    def lat_shard(s, k):
        return lat.at[s, c, span(k)]

    def lat_chip(k, slot):
        return to_chip(k, lat_shard(l, slot), lat_shard(l, slot), zg_s.at[k], lat_r.at[l, slot])

    def lat_layer(t, k):
        return to_layer(t, lat_shard(l, k), lat_shard(l, k), lf_s.at[t, k], lat_r.at[l, k])

    def lat_far(t, k):
        return remote(lat_shard(l, z), lat_shard(l, z), ld_s.at[t, k], lat_r.at[l, z], t, k * 2 + c)

    def lat_core(s):
        return to_core(lat.at[s, c], lat.at[s, c], co_s.at[s], co_r.at[s])

    def lat_wait(s, k):
        to_chip(z, lat_shard(s, k), lat_shard(s, k), zg_s.at[k], lat_r.at[s, k]).wait_recv()

    def own_latents():
        def add(j, total):
            k = far(chips - 2 - j)
            pre_copy(z, k).wait_recv()
            return total + qin[k].astype(F32)

        total = lax.fori_loop(0, chips - 1, add, pf[c, span(z)])
        lat[l, c, span(z)] = (act[...].astype(F32) * total).astype(BF16)
        peers(lambda k: lat_chip(k, z).start())
        peers(lambda k: if_distant(k, lambda: loop(l + 1, layers, lambda t: lat_far(t, k).start())))
        loop(l + 1, layers, lambda t: lat_layer(t, z).start())

    owned(z, own_latents)

    def pass_on(k):
        def step():
            lat_wait(l, k)
            if_close(k, lambda: loop(l + 1, layers, lambda t: lat_layer(t, k).start()))

        owned(k, step)

    peers_near_first(pass_on)
    lat_core(l).start()
    in_dec.wait()

    def whole(ref):
        return jnp.concatenate([ref[0], ref[1]], axis=1)

    def add_source(s):
        to_core(lat.at[s, other], lat.at[s, other], co_s.at[s], co_r.at[s]).wait_recv()
        recon[...] += jnp.dot(whole(lat.at[s]), dec[s], preferred_element_type=F32)

    def take_source(i):
        s = l - 1 - i
        loop(0, owners, lambda k: lat_wait(s, k))
        lat_core(s).start()
        add_source(s + 1)

    loop(0, l, take_source)
    add_source(0)
    err[...] = recon[...].astype(BF16)

    def term_core(s, h):
        return to_core(tb.at[s, h], tp.at[s], tp_s.at[s], tp_r.at[s])

    def make_term(s):
        term = lax.dot_general(
            err[...], dec[s], (((1,), (1,)), ((), ())), preferred_element_type=F32
        ).astype(BF16)
        tb[s, 0] = term[:, :half]
        tb[s, 1] = term[:, half:]
        term_core(s, other).start()

    loop(0, l + 1, make_term)

    def term_layer(s, t, k):
        return to_layer(s, cs.at[s, span(k)], tr.at[t, span(k)], tr_s.at[s, k], tr_r.at[t, k])

    def term_far(s, t, k, slot):
        return remote(cs.at[s, span(k)], td.at[t, slot], tr_s.at[s, k], td_r.at[t, slot], s, k * 2 + c)

    def start_term(s, k):
        if_close(k, term_layer(s, l, k).start)
        if_distant(k, term_far(s, l, k, z).start)

    def join_term(s):
        term_core(s, c).wait_recv()
        cs[s] = (tb[s, c].astype(F32) + tp[s].astype(F32)).astype(BF16)
        peers(lambda k: owned(k, lambda: start_term(s, k)))
        owned(z, term_layer(s, l, z).start)

    loop(0, l, join_term)
    term_core(l, c).wait_recv()
    lsf[...] = tb[l, c].astype(F32) + tp[l].astype(F32)

    def make_grad(s):
        dgv[s] = lax.dot_general(
            whole(lat.at[s]), err[...], (((0,), (0,)), ((), ())), preferred_element_type=F32
        )
        pltpu.make_async_copy(dgv.at[s], dg_hbm.at[0, s], dg_sem.at[s]).start()

    loop(0, l + 1, make_grad)

    def sum_copy(k, slot):
        return to_chip(k, ls.at[span(k)], zr.at[slot], z_s.at[k], z_r.at[slot])

    def layer_sum(k):
        def add(t, total):
            term_layer(l, t, k).wait_recv()
            return total + tr[t, span(k)].astype(F32)

        top = jnp.where(distant(k), l + 1, layers)
        return lax.fori_loop(l + 1, top, add, lsf[span(k)])

    def reduce_chip(k):
        def step():
            ls[span(k)] = layer_sum(k).astype(BF16)
            sum_copy(k, z).start()

        owned(k, step)

    peers(reduce_chip)

    def g_chip(k, slot):
        return to_chip(k, g.at[c, span(slot)], g.at[c, span(slot)], g_s.at[k], g_r.at[slot])

    def g_core(k, h):
        return to_core(g.at[h, span(k)], g.at[h, span(k)], gf_s.at[k], gf_r.at[k])

    def g_far(k):
        return remote(g.at[c, span(z)], g.at[c, span(z)], gd_s.at[k], gf_r.at[z], l, k * 2 + other)

    def own_grad():
        def add_far(k, total):
            def add(t, total):
                term_far(l, t, z, k).wait_recv()
                return total + td[t, k].astype(F32)

            top = jnp.where(distant(k), layers, l + 1)
            return lax.fori_loop(l + 1, top, add, total)

        def add(j, total):
            k = far(chips - 2 - j)
            sum_copy(z, k).wait_recv()
            return add_far(k, total + zr[k].astype(F32))

        total = lax.fori_loop(0, chips - 1, add, layer_sum(z))
        g[c, span(z)] = (act[...].astype(F32) * total).astype(BF16)
        peers(lambda k: g_chip(k, z).start())
        peers(lambda k: if_distant(k, g_far(k).start))
        g_core(z, c).start()

    owned(z, own_grad)

    def g_pass(k):
        def step():
            g_chip(z, k).wait_recv()
            if_close(k, g_core(k, c).start)

        owned(k, step)

    peers_near_first(g_pass)
    loop(0, owners, lambda k: g_core(k, other).wait_recv())
    egv[...] = lax.dot_general(
        x[...], whole(g), (((0,), (0,)), ((), ())), preferred_element_type=F32
    )
    out = pltpu.make_async_copy(egv, eg_hbm.at[0], eg_sem)
    out.start()

    pre_core.wait_send()
    peers(lambda k: owned(k, pre_copy(k, z).wait_send))

    def own_sends():
        peers(lambda k: lat_chip(k, z).wait_send())
        peers(lambda k: if_distant(k, lambda: loop(l + 1, layers, lambda t: lat_far(t, k).wait_send())))
        peers(lambda k: g_chip(k, z).wait_send())
        peers(lambda k: if_distant(k, g_far(k).wait_send))

    owned(z, own_sends)
    loop(0, owners, lambda k: if_close(k, lambda: loop(l + 1, layers, lambda t: lat_layer(t, k).wait_send())))
    loop(0, l + 1, lambda s: lat_core(s).wait_send())
    loop(0, l + 1, lambda s: term_core(s, other).wait_send())
    loop(0, l, lambda s: loop(0, owners, lambda k: term_layer(s, l, k).wait_send()))
    peers(lambda k: owned(k, sum_copy(k, z).wait_send))
    loop(0, owners, lambda k: if_close(k, g_core(k, c).wait_send))
    loop(0, layers, lambda s: pltpu.make_async_copy(dgv.at[s], dg_hbm.at[0, s], dg_sem.at[s]).wait())
    out.wait()


def body(x_in, enc_weight, active, dec_weight, target, other_sum):
    layers = lax.axis_size("layer")
    chips = lax.axis_size("dp") // 2
    _, tokens, width = x_in.shape
    features = enc_weight.shape[2]
    half = features // 2
    rows = 16 * pl.cdiv(tokens, 16 * chips)
    owners = tokens // rows
    assert owners * rows == tokens and owners <= chips
    dims = (layers, chips, owners, rows, tokens, half)

    def sems(*shape):
        return pltpu.SemaphoreType.DMA(shape) if shape else pltpu.SemaphoreType.DMA

    V = pltpu.VMEM
    scratch = [
        V((tokens, width), BF16), V((width, features), BF16), V((rows, half), jnp.int32),
        V((layers, features, width), BF16), V((tokens, width), BF16), V((tokens, width), BF16), sems(6),
        V((2, tokens, half), F32), V((tokens, half), BF16), V((tokens, half), BF16), sems(), sems(),
        V((tokens, half), BF16), V((chips, rows, half), BF16), sems(chips), sems(chips),
        V((layers, 2, tokens, half), BF16), sems(chips), sems(layers, chips), sems(layers, chips),
        sems(layers, chips),
        sems(layers), sems(layers),
        V((tokens, width), F32), V((tokens, width), BF16),
        V((layers, 2, tokens, half), BF16), V((layers, tokens, half), BF16), sems(layers), sems(layers),
        V((layers, tokens, half), BF16), V((layers, tokens, half), BF16), sems(layers, chips),
        sems(layers, chips), V((layers, chips, rows, half), BF16), sems(layers, chips), V((tokens, half), F32),
        V((tokens, half), BF16), V((chips, rows, half), BF16), sems(chips), sems(chips),
        V((2, tokens, half), BF16), sems(chips), sems(chips), sems(chips), sems(chips), sems(chips),
        V((layers, features, width), F32), V((width, features), F32), sems(layers), sems(),
    ]
    return pl.pallas_call(
        functools.partial(kernel, dims),
        out_shape=(
            jax.ShapeDtypeStruct((1, layers, features, width), F32),
            jax.ShapeDtypeStruct((1, width, features), F32),
        ),
        in_specs=[pl.BlockSpec(memory_space=pl.ANY)] * 6,
        out_specs=[pl.BlockSpec(memory_space=pl.ANY)] * 2,
        scratch_shapes=scratch,
        compiler_params=pltpu.CompilerParams(
            collective_id=0, has_side_effects=True, vmem_limit_bytes=63 * 1024 * 1024
        ),
    )(x_in, enc_weight, active, dec_weight, target, other_sum)


def solution(mesh):
    return jax.shard_map(
        body,
        mesh=mesh,
        in_specs=(
            P("layer", None, "dp"),
            P("layer", "dp", None),
            P("layer", None, None),
            P("layer", None, None, "dp"),
            P("layer", None, "dp"),
            P("layer", None, "dp"),
        ),
        out_specs=(P("layer", None, None, "dp"), P("layer", "dp", None)),
        check_vma=False,
    )
```

```python
import functools

import jax
import jax.numpy as jnp
from jax import lax
from jax.experimental import pallas as pl
from jax.experimental.pallas import tpu as pltpu
from jax.sharding import PartitionSpec as P

BF16 = jnp.bfloat16
F32 = jnp.float32
LAT = ()
TERM = ()
GRAD = ()


def loop(low, high, step):
    def one(index, carry):
        step(index)
        return carry

    lax.fori_loop(low, high, one, 0)


def kernel(
    dims, x_hbm, enc_hbm, act_hbm, dec_hbm, tgt_hbm, oth_hbm, dg_hbm, eg_hbm,
    x, enc, act, dec, tgt, oth, in_sem,
    pf, pb, pin, p_s, p_r,
    qs, qin, q_s, q_r,
    lat, zg_s, lf_s, ld_s, lat_r, co_s, co_r,
    recon, err,
    tb, tp, tp_s, tp_r,
    cs, tr, tr_s, tr_r, td, td_r, lsf,
    ls, zr, z_s, z_r,
    g, g_s, g_r, gf_s, gf_r, gd_s,
    dgv, egv, dg_sem, eg_sem,
):
    layers, chips, owners, rows, tokens, half = dims
    l = lax.axis_index("layer")
    d = lax.axis_index("dp")
    z = lax.div(d, 2)
    c = lax.rem(d, 2)
    other = 1 - c

    def owned(index, step):
        if owners == chips:
            step()
        else:
            pl.when(index < owners)(step)

    def span(k):
        return pl.ds(pl.multiple_of(k * rows, 16), rows)

    lower = 2 * z < chips
    place = jnp.where(lower, chips - 1 - z, z)

    def far(j):
        j = j + jnp.where(j >= place, 1, 0)
        return jnp.where(lower, chips - 1 - j, j)

    def peers(step):
        loop(0, chips - 1, lambda j: step(far(j)))

    def peers_near_first(step):
        loop(0, chips - 1, lambda j: step(far(chips - 2 - j)))

    def among(k, steps):
        gap = jnp.abs(k - z)
        found = gap < 0
        for step in steps:
            found = jnp.logical_or(found, gap == step)
        return found

    def if_direct(k, steps, action):
        if steps:
            pl.when(among(k, steps))(action)

    def if_relayed(k, steps, action):
        if steps:
            pl.when(jnp.logical_not(among(k, steps)))(action)
        else:
            action()

    direct = tuple(sorted({*LAT, *TERM, *GRAD}))
    far_count = 0
    for gap in direct:
        far_count = far_count + jnp.where(z >= gap, 1, 0) + jnp.where(z + gap < chips, 1, 0)

    def remote(src, dst, send, recv, layer, part):
        return pltpu.make_async_remote_copy(
            src_ref=src, dst_ref=dst, send_sem=send, recv_sem=recv,
            device_id=(layer, part), device_id_type=pl.DeviceIdType.MESH,
        )

    def to_core(src, dst, send, recv):
        return remote(src, dst, send, recv, l, z * 2 + other)

    def to_chip(k, src, dst, send, recv):
        return remote(src, dst, send, recv, l, k * 2 + c)

    def to_layer(t, src, dst, send, recv):
        return remote(src, dst, send, recv, t, d)

    barrier = pltpu.get_barrier_semaphore()

    def greet(layer, part):
        pl.semaphore_signal(
            barrier, inc=1, device_id=(layer, part), device_id_type=pl.DeviceIdType.MESH
        )

    greet(l, z * 2 + other)
    peers(lambda k: greet(l, k * 2 + c))
    loop(1, layers, lambda i: greet(lax.rem(l + i, layers), d))

    def greet_distant(k):
        greet(l, k * 2 + other)
        loop(1, layers, lambda i: greet(lax.rem(l + i, layers), k * 2 + c))

    peers(lambda k: if_direct(k, direct, lambda: greet_distant(k)))

    in_x = pltpu.make_async_copy(x_hbm.at[0], x, in_sem.at[0])
    in_enc = pltpu.make_async_copy(enc_hbm.at[0], enc, in_sem.at[1])
    in_dec = pltpu.make_async_copy(dec_hbm.at[0], dec, in_sem.at[2])
    in_tgt = pltpu.make_async_copy(tgt_hbm.at[0], tgt, in_sem.at[3])
    in_oth = pltpu.make_async_copy(oth_hbm.at[0], oth, in_sem.at[4])
    in_act = pltpu.make_async_copy(
        act_hbm.at[0, span(z), pl.ds(pl.multiple_of(c * half, 128), half)], act, in_sem.at[5]
    )
    in_x.start()
    in_enc.start()
    owned(z, in_act.start)
    in_oth.start()
    in_tgt.start()
    in_dec.start()

    in_x.wait()
    in_enc.wait()
    part = jnp.dot(x[...], enc[...], preferred_element_type=F32)
    pf[0] = part[:, :half]
    pf[1] = part[:, half:]
    pb[...] = pf[other].astype(BF16)
    pl.semaphore_wait(barrier, chips + layers - 1 + far_count * layers)

    pre_core = to_core(pb, pin, p_s, p_r)
    pre_core.start()

    def clear(s):
        dgv[s] = jnp.zeros_like(dgv[s])
        pltpu.make_async_copy(dgv.at[s], dg_hbm.at[0, s], dg_sem.at[s]).start()

    loop(l + 1, layers, clear)
    owned(z, in_act.wait)
    in_oth.wait()
    in_tgt.wait()
    recon[...] = oth[...].astype(F32) - tgt[...].astype(F32)
    pre_core.wait_recv()
    pf[c] = pf[c] + pin[...].astype(F32)
    qs[...] = pf[c].astype(BF16)

    def pre_copy(k, slot):
        return to_chip(k, qs.at[span(k)], qin.at[slot], q_s.at[k], q_r.at[slot])

    peers(lambda k: owned(k, pre_copy(k, z).start))

    def lat_shard(s, k):
        return lat.at[s, c, span(k)]

    def lat_chip(k, slot):
        return to_chip(k, lat_shard(l, slot), lat_shard(l, slot), zg_s.at[k], lat_r.at[l, slot])

    def lat_layer(t, k):
        return to_layer(t, lat_shard(l, k), lat_shard(l, k), lf_s.at[t, k], lat_r.at[l, k])

    def lat_far(t, k):
        return remote(lat_shard(l, z), lat_shard(l, z), ld_s.at[t, k], lat_r.at[l, z], t, k * 2 + c)

    def lat_core(s):
        return to_core(lat.at[s, c], lat.at[s, c], co_s.at[s], co_r.at[s])

    def lat_wait(s, k):
        to_chip(z, lat_shard(s, k), lat_shard(s, k), zg_s.at[k], lat_r.at[s, k]).wait_recv()

    def own_latents():
        def add(j, total):
            k = far(chips - 2 - j)
            pre_copy(z, k).wait_recv()
            return total + qin[k].astype(F32)

        total = lax.fori_loop(0, chips - 1, add, pf[c, span(z)])
        lat[l, c, span(z)] = (act[...].astype(F32) * total).astype(BF16)
        peers(lambda k: lat_chip(k, z).start())
        peers(lambda k: if_direct(k, LAT, lambda: loop(l + 1, layers, lambda t: lat_far(t, k).start())))
        loop(l + 1, layers, lambda t: lat_layer(t, z).start())

    owned(z, own_latents)

    def pass_on(k):
        def step():
            lat_wait(l, k)
            if_relayed(k, LAT, lambda: loop(l + 1, layers, lambda t: lat_layer(t, k).start()))

        owned(k, step)

    peers_near_first(pass_on)
    lat_core(l).start()
    in_dec.wait()

    def whole(ref):
        return jnp.concatenate([ref[0], ref[1]], axis=1)

    def add_source(s):
        to_core(lat.at[s, other], lat.at[s, other], co_s.at[s], co_r.at[s]).wait_recv()
        recon[...] += jnp.dot(whole(lat.at[s]), dec[s], preferred_element_type=F32)

    def take_source(i):
        s = l - 1 - i
        loop(0, owners, lambda k: lat_wait(s, k))
        lat_core(s).start()
        add_source(s + 1)

    loop(0, l, take_source)
    add_source(0)
    err[...] = recon[...].astype(BF16)

    def term_core(s, h):
        return to_core(tb.at[s, h], tp.at[s], tp_s.at[s], tp_r.at[s])

    def make_term(s):
        term = lax.dot_general(
            err[...], dec[s], (((1,), (1,)), ((), ())), preferred_element_type=F32
        ).astype(BF16)
        tb[s, 0] = term[:, :half]
        tb[s, 1] = term[:, half:]
        term_core(s, other).start()

    loop(0, l + 1, make_term)

    def term_layer(s, t, k):
        return to_layer(s, cs.at[s, span(k)], tr.at[t, span(k)], tr_s.at[s, k], tr_r.at[t, k])

    def term_far(s, t, k, slot):
        return remote(cs.at[s, span(k)], td.at[t, slot], tr_s.at[s, k], td_r.at[t, slot], s, k * 2 + c)

    def start_term(s, k):
        if_relayed(k, TERM, term_layer(s, l, k).start)
        if_direct(k, TERM, term_far(s, l, k, z).start)

    def join_term(s):
        term_core(s, c).wait_recv()
        cs[s] = (tb[s, c].astype(F32) + tp[s].astype(F32)).astype(BF16)
        peers(lambda k: owned(k, lambda: start_term(s, k)))
        owned(z, term_layer(s, l, z).start)

    loop(0, l, join_term)
    term_core(l, c).wait_recv()
    lsf[...] = tb[l, c].astype(F32) + tp[l].astype(F32)

    def make_grad(s):
        dgv[s] = lax.dot_general(
            whole(lat.at[s]), err[...], (((0,), (0,)), ((), ())), preferred_element_type=F32
        )
        pltpu.make_async_copy(dgv.at[s], dg_hbm.at[0, s], dg_sem.at[s]).start()

    loop(0, l + 1, make_grad)

    def sum_copy(k, slot):
        return to_chip(k, ls.at[span(k)], zr.at[slot], z_s.at[k], z_r.at[slot])

    def layer_sum(k):
        def add(t, total):
            term_layer(l, t, k).wait_recv()
            return total + tr[t, span(k)].astype(F32)

        top = jnp.where(among(k, TERM), l + 1, layers)
        return lax.fori_loop(l + 1, top, add, lsf[span(k)])

    def reduce_chip(k):
        def step():
            ls[span(k)] = layer_sum(k).astype(BF16)
            sum_copy(k, z).start()

        owned(k, step)

    peers(reduce_chip)

    def g_chip(k, slot):
        return to_chip(k, g.at[c, span(slot)], g.at[c, span(slot)], g_s.at[k], g_r.at[slot])

    def g_core(k, h):
        return to_core(g.at[h, span(k)], g.at[h, span(k)], gf_s.at[k], gf_r.at[k])

    def g_far(k):
        return remote(g.at[c, span(z)], g.at[c, span(z)], gd_s.at[k], gf_r.at[z], l, k * 2 + other)

    def own_grad():
        def add_far(k, total):
            def add(t, total):
                term_far(l, t, z, k).wait_recv()
                return total + td[t, k].astype(F32)

            top = jnp.where(among(k, TERM), layers, l + 1)
            return lax.fori_loop(l + 1, top, add, total)

        def add(j, total):
            k = far(chips - 2 - j)
            sum_copy(z, k).wait_recv()
            return add_far(k, total + zr[k].astype(F32))

        total = lax.fori_loop(0, chips - 1, add, layer_sum(z))
        g[c, span(z)] = (act[...].astype(F32) * total).astype(BF16)
        peers(lambda k: g_chip(k, z).start())
        peers(lambda k: if_direct(k, GRAD, g_far(k).start))
        g_core(z, c).start()

    owned(z, own_grad)

    def g_pass(k):
        def step():
            g_chip(z, k).wait_recv()
            if_relayed(k, GRAD, g_core(k, c).start)

        owned(k, step)

    peers_near_first(g_pass)
    def enc_part(h):
        lanes = pl.ds(pl.multiple_of(h * half, 128), half)
        egv[:, lanes] = lax.dot_general(
            x[...], g[h], (((0,), (0,)), ((), ())), preferred_element_type=F32
        )
        return pltpu.make_async_copy(egv.at[:, lanes], eg_hbm.at[0, :, lanes], eg_sem.at[h])

    out_own = enc_part(c)
    out_own.start()
    loop(0, owners, lambda k: g_core(k, other).wait_recv())
    out_other = enc_part(other)
    out_other.start()

    pre_core.wait_send()
    peers(lambda k: owned(k, pre_copy(k, z).wait_send))

    def own_sends():
        peers(lambda k: lat_chip(k, z).wait_send())
        peers(lambda k: if_direct(k, LAT, lambda: loop(l + 1, layers, lambda t: lat_far(t, k).wait_send())))
        peers(lambda k: g_chip(k, z).wait_send())
        peers(lambda k: if_direct(k, GRAD, g_far(k).wait_send))

    owned(z, own_sends)
    loop(0, owners, lambda k: if_relayed(k, LAT, lambda: loop(l + 1, layers, lambda t: lat_layer(t, k).wait_send())))
    loop(0, l + 1, lambda s: lat_core(s).wait_send())
    loop(0, l + 1, lambda s: term_core(s, other).wait_send())
    loop(0, l, lambda s: loop(0, owners, lambda k: term_layer(s, l, k).wait_send()))
    peers(lambda k: owned(k, sum_copy(k, z).wait_send))
    loop(0, owners, lambda k: if_relayed(k, GRAD, g_core(k, c).wait_send))
    loop(0, layers, lambda s: pltpu.make_async_copy(dgv.at[s], dg_hbm.at[0, s], dg_sem.at[s]).wait())
    out_own.wait()
    out_other.wait()


def body(x_in, enc_weight, active, dec_weight, target, other_sum):
    layers = lax.axis_size("layer")
    chips = lax.axis_size("dp") // 2
    _, tokens, width = x_in.shape
    features = enc_weight.shape[2]
    half = features // 2
    rows = 16 * pl.cdiv(tokens, 16 * chips)
    owners = tokens // rows
    assert owners * rows == tokens and owners <= chips
    dims = (layers, chips, owners, rows, tokens, half)

    def sems(*shape):
        return pltpu.SemaphoreType.DMA(shape) if shape else pltpu.SemaphoreType.DMA

    V = pltpu.VMEM
    scratch = [
        V((tokens, width), BF16), V((width, features), BF16), V((rows, half), jnp.int32),
        V((layers, features, width), BF16), V((tokens, width), BF16), V((tokens, width), BF16), sems(6),
        V((2, tokens, half), F32), V((tokens, half), BF16), V((tokens, half), BF16), sems(), sems(),
        V((tokens, half), BF16), V((chips, rows, half), BF16), sems(chips), sems(chips),
        V((layers, 2, tokens, half), BF16), sems(chips), sems(layers, chips), sems(layers, chips),
        sems(layers, chips),
        sems(layers), sems(layers),
        V((tokens, width), F32), V((tokens, width), BF16),
        V((layers, 2, tokens, half), BF16), V((layers, tokens, half), BF16), sems(layers), sems(layers),
        V((layers, tokens, half), BF16), V((layers, tokens, half), BF16), sems(layers, chips),
        sems(layers, chips), V((layers, chips, rows, half), BF16), sems(layers, chips), V((tokens, half), F32),
        V((tokens, half), BF16), V((chips, rows, half), BF16), sems(chips), sems(chips),
        V((2, tokens, half), BF16), sems(chips), sems(chips), sems(chips), sems(chips), sems(chips),
        V((layers, features, width), F32), V((width, features), F32), sems(layers), sems(2),
    ]
    return pl.pallas_call(
        functools.partial(kernel, dims),
        out_shape=(
            jax.ShapeDtypeStruct((1, layers, features, width), F32),
            jax.ShapeDtypeStruct((1, width, features), F32),
        ),
        in_specs=[pl.BlockSpec(memory_space=pl.ANY)] * 6,
        out_specs=[pl.BlockSpec(memory_space=pl.ANY)] * 2,
        scratch_shapes=scratch,
        compiler_params=pltpu.CompilerParams(
            collective_id=0, has_side_effects=True, vmem_limit_bytes=63 * 1024 * 1024
        ),
    )(x_in, enc_weight, active, dec_weight, target, other_sum)


def solution(mesh):
    return jax.shard_map(
        body,
        mesh=mesh,
        in_specs=(
            P("layer", None, "dp"),
            P("layer", "dp", None),
            P("layer", None, None),
            P("layer", None, None, "dp"),
            P("layer", None, "dp"),
            P("layer", None, "dp"),
        ),
        out_specs=(P("layer", None, None, "dp"), P("layer", "dp", None)),
        check_vma=False,
    )
```
